128 devices in a mesh: ctx: 32 (over x, y_lo, z), head: 4 (over y_hi, core).
Axes of the slice: x: 4, y: 4 (y_hi: 2, y_lo: 2; y = y_hi * 2 + y_lo), z: 4, core: 2. Of those that a mesh axis runs over, the one named last changes fastest.
Arguments:
- queries: bfloat16 [32768, 1024], P('ctx', 'head'), may hold values from -18 to 18
- keys: bfloat16 [32768, 128], P('ctx'), may hold values from -6 to 6
- values: bfloat16 [32768, 128], P('ctx'), may hold values from -6 to 6
- grad_out: bfloat16 [32768, 1024], P('ctx', 'head'), may hold values from -6 to 6
- lengths: int32 [128], replicated, may hold values from 1 to 4096, 32768 in all
Outputs:
- attn_out: bfloat16 [32768, 1024], P('ctx', 'head')
- grad_queries: bfloat16 [32768, 1024], P('ctx', 'head')
- grad_keys: bfloat16 [32768, 128], P(('ctx', 'head'))
- grad_values: bfloat16 [32768, 128], P(('ctx', 'head'))
The draws below stay inside these ranges and needn't reach their ends.
Inputs may be any that keep to these rules, and one draw needn't show every extreme that they name: The lengths sum to 32768; one response has exactly 4096 tokens.
All inputs are finite; a program needn't handle non-finite values.
Results may differ from the reference program's by a relative error of at most 0.0072.
Values may be sent and summed in bfloat16 or wider, within the bound.
No kernel may reach another device: no remote copies, remote signals or barrier semaphores. Data moves between devices by JAX's collectives and lax.ppermute only.
A program may use at most 192 MiB of HBM per device.

```python
import math
import jax
import jax.numpy as jnp
import numpy as np
from jax import lax

HEADS = 8
DH = 128
TOK_DEV = 1024
SPAN = 4
TOKENS = 32768
MAXLEN = 4096
NDOCS = 128


def drawn_pair(key):
    base = jax.random.fold_in(key, 4242)
    query_key, keys_key = jax.random.split(base, 2)
    query_rows = jnp.clip(jax.random.normal(query_key, (TOKENS, HEADS * DH), jnp.float32), -6.0, 6.0)
    key_rows = jnp.clip(jax.random.normal(keys_key, (TOKENS, DH), jnp.float32), -6.0, 6.0)
    return (query_rows, key_rows)


def draw_queries(key, part):
    return drawn_pair(key)[0].astype(jnp.bfloat16)


def draw_keys(key, part):
    return drawn_pair(key)[1].astype(jnp.bfloat16)


def block_levels(stream_key, shape, pieces, least, top_value):
    def one(position, shards_of):
        draws = jax.random.uniform(jax.random.fold_in(jax.random.fold_in(stream_key, 6), position), (shards_of,), jnp.float32, least / len(pieces), top_value / len(pieces))
        return jnp.repeat(jnp.exp(draws), shape[position] // shards_of).reshape((-1,) + (1,) * (len(shape) - position - 1))

    loudness = one(*pieces[0])
    for cut in pieces[1:]:
        loudness = loudness * one(*cut)
    return loudness


def split_up(count, total, bound, slope):
    portions = [(1 << 20) // math.isqrt(grade ** slope) + 1 for grade in range(2, count + 1)]
    spare, given = total - bound - (count - 1), [1] * (count - 1)
    while spare > 0:
        candidates = [i for i in range(count - 1) if given[i] < bound]
        mass, budget = sum([portions[i] for i in candidates]), spare
        for i in candidates:
            addition = min(bound - given[i], max(1, budget * portions[i] // mass), spare)
            given[i] = given[i] + addition
            spare = spare - addition
    return np.array([bound] + given)


def uneven_parts(rng, number_of, total, reach, skew):
    if number_of == 2:
        one = jax.random.randint(rng, (), max(1, total - reach), min(reach, total - 1) + 1)
        return jnp.stack([one, total - one])
    tallies = jnp.asarray(split_up(number_of, total, reach, skew), jnp.int32)
    pairs = (number_of - 1) // 2
    donor, receiver = tallies[1:1 + 2 * pairs:2], tallies[2:2 + 2 * pairs:2]
    slack = jnp.minimum(donor - 1, reach - receiver)
    moved = jax.random.randint(jax.random.fold_in(rng, 1), (pairs,), 0, 1 << 20) % (slack + 1)
    tallies = tallies.at[1:1 + 2 * pairs:2].set(donor - moved).at[2:2 + 2 * pairs:2].set(receiver + moved)
    return tallies[jax.random.permutation(jax.random.fold_in(rng, 2), number_of)]


def gaussian(own_key, extent, scale, limit, cuts=(), held_as=jnp.bfloat16):
    entries = scale * jax.random.normal(own_key, extent, jnp.float32)
    if cuts:
        entries = entries * block_levels(own_key, extent, cuts, -0.22, 0.18)
    return jnp.clip(entries, -limit, limit).astype(held_as)


def setup_inputs(seed: int = 0) -> dict:
    key_list = jax.random.split(jax.random.key(seed), 6)
    return {
        "queries": draw_queries(jax.random.fold_in(key_list[5], 71), 0),
        "keys": draw_keys(jax.random.fold_in(key_list[5], 71), 0),
        "values": gaussian(key_list[2], (TOKENS, DH), 1.0, 6.0, ((0, 32),)),
        "grad_out": gaussian(key_list[3], (TOKENS, HEADS * DH), 1.0, 6.0, ((0, 32), (1, 4))),
        "lengths": uneven_parts(key_list[4], NDOCS, TOKENS, MAXLEN, 2).astype(jnp.int32),
    }


masked_score = -1e+30

def reference(queries, keys, values, grad_out, lengths):
    spread = 1.0 / math.sqrt(DH)
    window = SPAN * TOK_DEV
    span_rows = window + TOK_DEV
    cumulative = jnp.cumsum(lengths).astype(jnp.int32)
    positions = jnp.arange(TOKENS, dtype=jnp.int32)
    docs = lax.optimization_barrier(jnp.sum((cumulative[None, :] <= positions[:, None]).astype(jnp.int32), axis=1)).astype(jnp.int32)
    key_pos_all = jnp.concatenate([jnp.arange(-window, 0, dtype=jnp.int32), positions])
    key_doc_all = jnp.concatenate([jnp.full((window,), -1, jnp.int32), docs])
    key_pad = jnp.concatenate([jnp.zeros((window, DH), jnp.float32), keys.astype(jnp.float32)])
    value_pad = jnp.concatenate([jnp.zeros((window, DH), jnp.float32), values.astype(jnp.float32)])
    queries3 = queries.astype(jnp.float32).reshape(TOKENS, HEADS, DH)
    grads3 = grad_out.astype(jnp.float32).reshape(TOKENS, HEADS, DH)

    def step(carry, index):
        key_grad, value_grad = carry
        start = (index * TOK_DEV).astype(jnp.int32)
        query_block = lax.dynamic_slice_in_dim(queries3, start, TOK_DEV, 0)
        grad_block = lax.dynamic_slice_in_dim(grads3, start, TOK_DEV, 0)
        query_pos = lax.dynamic_slice_in_dim(positions, start, TOK_DEV, 0)
        query_doc = lax.dynamic_slice_in_dim(docs, start, TOK_DEV, 0)
        kmatrix = lax.dynamic_slice_in_dim(key_pad, start, span_rows, 0)
        vmatrix = lax.dynamic_slice_in_dim(value_pad, start, span_rows, 0)
        key_pos = lax.dynamic_slice_in_dim(key_pos_all, start, span_rows, 0)
        key_doc = lax.dynamic_slice_in_dim(key_doc_all, start, span_rows, 0)
        scaled = jnp.einsum('qhd,kd->hqk', query_block, kmatrix) * spread
        visible = (query_doc[:, None] == key_doc[None, :]) & (key_pos[None, :] <= query_pos[:, None])
        scores = jnp.where(visible[None], scaled, masked_score)
        highest = lax.optimization_barrier(jnp.max(scores, axis=2))
        row_lse = highest + jnp.log(lax.optimization_barrier(jnp.sum(jnp.exp(scores - highest[..., None]), axis=2)))
        probs = jnp.exp(scores - row_lse[..., None])
        probs_low = lax.optimization_barrier(probs.astype(jnp.bfloat16)).astype(jnp.float32)
        out32 = jnp.einsum('hqk,kd->qhd', probs_low, vmatrix)
        delta = lax.optimization_barrier(jnp.sum(grad_block * out32, axis=2)).T
        dprob = jnp.einsum('qhd,kd->hqk', grad_block, vmatrix)
        dscore = probs * (dprob - delta[..., None])
        dscore = lax.optimization_barrier(dscore.astype(jnp.bfloat16)).astype(jnp.float32)
        query_grad = jnp.einsum('hqk,kd->qhd', dscore, kmatrix) * spread
        key_part = jnp.einsum('hqk,qhd->kd', dscore, query_block) * spread
        value_part = jnp.einsum('hqk,qhd->kd', probs_low, grad_block)
        key_grad = lax.dynamic_update_slice_in_dim(key_grad, lax.dynamic_slice_in_dim(key_grad, start, span_rows, 0) + key_part, start, 0)
        value_grad = lax.dynamic_update_slice_in_dim(value_grad, lax.dynamic_slice_in_dim(value_grad, start, span_rows, 0) + value_part, start, 0)
        return ((key_grad, value_grad), (out32.astype(jnp.bfloat16), query_grad.astype(jnp.bfloat16)))
    start_state = (jnp.zeros((window + TOKENS, DH), jnp.float32), jnp.zeros((window + TOKENS, DH), jnp.float32))
    (key_grad, value_grad), (outputs, query_grads) = lax.scan(step, start_state, jnp.arange(TOKENS // TOK_DEV, dtype=jnp.int32))
    attn_out = outputs.reshape(TOKENS, HEADS * DH)
    grad_queries = query_grads.reshape(TOKENS, HEADS * DH)
    return (attn_out, grad_queries, key_grad[window:].astype(jnp.bfloat16), value_grad[window:].astype(jnp.bfloat16))
```

```python
import math

import jax
import jax.numpy as jnp
from jax import lax
from jax.experimental import pallas as pl
from jax.experimental.pallas import tpu as pltpu
from jax.sharding import PartitionSpec as P

DH = 128
SPAN = 4
ROWS = 1024
WIN = (SPAN + 1) * ROWS
HL = 2
BQ = 512
BK = 512
M = HL * BQ
QUARTER = ROWS // 4
masked_score = -1e30
F32 = jnp.float32
BF16 = jnp.bfloat16
ROW_ROW = (((1,), (1,)), ((), ()))
ROW_COL = (((1,), (0,)), ((), ()))


def dot(a, b, dims):
    return lax.dot_general(a, b, dims, preferred_element_type=F32)


def attn_kernel(sc_ref, begin_ref, q_ref, g_ref, k_hbm, v_hbm, *rest):
    mine = rest[:SPAN]
    other = rest[SPAN : 2 * SPAN]
    o_ref, dq_ref, send_ref, keep_ref = rest[2 * SPAN : 2 * SPAN + 4]
    kv, kt, vt, s_scr, dk, dv, ot_s, dq_s, g_s, q_s, stage, sem, out_sem = rest[2 * SPAN + 4 :]
    nq = ROWS // BQ
    core = sc_ref[2 * nq]
    kw = kv.at[0]
    vw = kv.at[1]
    copies = []
    for src, side, d in (
        [(k_hbm, 0, 0), (v_hbm, 1, 0)]
        + [(mine[d - 1], core, d) for d in range(1, SPAN + 1)]
        + [(other[d - 1], 1 - core, d) for d in range(1, SPAN + 1)]
    ):
        dst = kv.at[side, pl.ds((SPAN - d) * ROWS, ROWS), :]
        copies.append(pltpu.make_async_copy(src, dst, sem.at[len(copies)]))
    for c in copies:
        c.start()
    dk[...] = jnp.zeros_like(dk)
    dv[...] = jnp.zeros_like(dv)
    for c in copies:
        c.wait()

    def krow(j):
        return pl.ds(pl.multiple_of(j * BK, BK), BK)

    @pl.loop(sc_ref[0] // BK, WIN // BK)
    def _(j):
        kt[:, krow(j)] = kw[krow(j), :].T
        vt[:, krow(j)] = vw[krow(j), :].T

    fac = 1.0 / math.sqrt(DH)
    c2 = math.log2(math.e) * fac

    @pl.loop(0, nq)
    def _(qb):
        qr = pl.ds(pl.multiple_of(qb * BQ, BQ), BQ)
        for h in range(HL):
            q_s[h * BQ : (h + 1) * BQ, :] = q_ref[qr, h * DH : (h + 1) * DH]
        diag = (SPAN * ROWS) // BK + qb
        lo = sc_ref[qb] // BK
        full = jnp.minimum((sc_ref[nq + qb] + BK - 1) // BK, diag)
        beg = jnp.concatenate([begin_ref[:, qr]] * HL, axis=1)

        def score(j, m, masked):
            s = dot(kw[krow(j), :], q_s[...], ROW_ROW)
            if masked:
                kp = j * BK + lax.broadcasted_iota(jnp.int32, (BK, M), 0)
                qp = diag * BK + (lax.broadcasted_iota(jnp.int32, (1, M), 1) & (BQ - 1))
                s = jnp.where((kp >= beg) & (kp <= qp), s, masked_score)
            s_scr[krow(j), :] = s
            return jnp.maximum(m, jnp.max(s.reshape(BK // 8, 8, M), axis=0))

        def masked_body(i, m):
            return score(jnp.where(i == 0, diag, lo + i - 1), m, True)

        m = jnp.full((8, M), masked_score, F32)
        m = lax.fori_loop(0, 1 + full - lo, masked_body, m)
        m = lax.fori_loop(full, diag, lambda j, m: score(j, m, False), m)
        top = jnp.max(m, axis=0, keepdims=True) * c2
        ot_s[...] = jnp.zeros_like(ot_s)
        dq_s[...] = jnp.zeros_like(dq_s)

        def forward_body(j, total):
            p = jnp.exp2(s_scr[krow(j), :] * c2 - top)
            s_scr[krow(j), :] = p
            ot_s[...] += dot(vt[:, krow(j)], p.astype(BF16), ROW_COL)
            return total + jnp.sum(p.reshape(BK // 8, 8, M), axis=0)

        total = lax.fori_loop(lo, diag + 1, forward_body, jnp.zeros((8, M), F32))
        inv = 1.0 / jnp.sum(total, axis=0, keepdims=True)
        out_t = ot_s[...] * inv
        g_t = jnp.concatenate([g_ref[qr, h * DH : (h + 1) * DH].T for h in range(HL)], axis=1)
        g_t = (g_t.astype(F32) * inv).astype(BF16)
        g_s[...] = g_t.T
        out_low = out_t.astype(BF16)
        for h in range(HL):
            o_ref[qr, h * DH : (h + 1) * DH] = out_low[:, h * BQ : (h + 1) * BQ].T
        delta = jnp.sum(g_t.astype(F32) * out_t, axis=0, keepdims=True)

        def backward_body(j, carry):
            kr = krow(j)
            dp = dot(vw[kr, :], g_s[...], ROW_ROW)
            p = s_scr[kr, :]
            ds = (p * (dp - delta)).astype(BF16)
            dq_s[...] += dot(kt[:, kr], ds, ROW_COL)
            dk[kr, :] += dot(ds, q_s[...], ROW_COL)
            dv[kr, :] += dot(p.astype(BF16), g_s[...], ROW_COL)
            return carry

        lax.fori_loop(lo, diag + 1, backward_body, 0)
        dq_low = (dq_s[...] * fac).astype(BF16)
        for h in range(HL):
            dq_ref[qr, h * DH : (h + 1) * DH] = dq_low[:, h * BQ : (h + 1) * BQ].T

    outs = []
    for side, dst in ((1 - core, send_ref), (core, keep_ref)):
        for w in range(SPAN + 1):
            slot = len(outs)
            for t in range(2):
                start = pl.multiple_of(w * ROWS + (2 * t + side) * QUARTER, QUARTER)
                rows = pl.ds(start, QUARTER)
                stage[slot, t, :, 0:DH] = (dk[rows, :] * fac).astype(BF16)
                stage[slot, t, :, DH : 2 * DH] = dv[rows, :].astype(BF16)
            outs.append(pltpu.make_async_copy(stage.at[slot], dst.at[w], out_sem.at[slot]))
            outs[-1].start()
    for c in outs:
        c.wait()


def attention(scalars, begin, q, g, k, v, mine, other):
    anywhere = pl.BlockSpec(memory_space=pl.ANY)
    vmem = pl.BlockSpec(memory_space=pltpu.VMEM)
    part = (SPAN + 1, 2, QUARTER, 2 * DH)
    return pl.pallas_call(
        attn_kernel,
        out_shape=(
            jax.ShapeDtypeStruct((ROWS, HL * DH), BF16),
            jax.ShapeDtypeStruct((ROWS, HL * DH), BF16),
            jax.ShapeDtypeStruct(part, BF16),
            jax.ShapeDtypeStruct(part, BF16),
        ),
        in_specs=[pl.BlockSpec(memory_space=pltpu.SMEM), vmem, vmem, vmem]
        + [anywhere] * (2 + 2 * SPAN),
        out_specs=(vmem, vmem, anywhere, anywhere),
        scratch_shapes=[
            pltpu.VMEM((2, WIN, DH), BF16),
            pltpu.VMEM((DH, WIN), BF16),
            pltpu.VMEM((DH, WIN), BF16),
            pltpu.VMEM((WIN, M), F32),
            pltpu.VMEM((WIN, DH), F32),
            pltpu.VMEM((WIN, DH), F32),
            pltpu.VMEM((DH, M), F32),
            pltpu.VMEM((DH, M), F32),
            pltpu.VMEM((M, DH), BF16),
            pltpu.VMEM((M, DH), BF16),
            pltpu.VMEM((2 * (SPAN + 1), 2, QUARTER, 2 * DH), BF16),
            pltpu.SemaphoreType.DMA((2 + 2 * SPAN,)),
            pltpu.SemaphoreType.DMA((2 * (SPAN + 1),)),
        ],
        compiler_params=pltpu.CompilerParams(vmem_limit_bytes=60 * 2**20),
        name="attn",
    )(scalars, begin, q, g, k, v, *mine, *other)


def along_ctx(x, by):
    count = lax.axis_size("ctx")
    return lax.ppermute(x, "ctx", [(i, (i + by) % count) for i in range(count)])


def along_head(x, flip):
    return lax.ppermute(x, "head", [(i, i ^ flip) for i in range(4)])


def shards(queries, keys, values, grad_out, lengths):
    place = lax.axis_index("ctx")
    head = lax.axis_index("head")
    core = head % 2
    side = head // 2
    carried = jnp.where(core == 0, keys, values)
    mine = [along_ctx(carried, d) for d in range(1, SPAN + 1)]
    other = [along_head(x, 1) for x in mine]

    docs = jnp.arange(lengths.shape[0])
    ends = jnp.sum(jnp.where(docs[None, :] <= docs[:, None], lengths[None, :], 0), axis=1)
    own = place * ROWS + jnp.arange(ROWS, dtype=jnp.int32)
    begin = jnp.max(jnp.where(ends[:, None] <= own[None, :], ends[:, None], 0), axis=0)
    begin = begin - (place - SPAN) * ROWS
    scalars = jnp.concatenate([begin[::BQ], begin[BQ - 1 :: BQ], core[None]]).astype(jnp.int32)

    out, grad_q, send, keep = attention(
        scalars, begin.reshape(1, ROWS), queries, grad_out, keys, values, mine, other
    )
    swapped = along_head(send, 1)
    totals = [
        keep[SPAN - d].astype(F32) + swapped[SPAN - d].astype(F32) for d in range(SPAN + 1)
    ]
    acc = totals[0]
    for d in range(1, SPAN + 1):
        acc = acc + along_ctx(totals[d].astype(BF16), -d).astype(F32)
    give = lax.dynamic_index_in_dim(acc, 1 - side, 0, keepdims=False).astype(BF16)
    stay = lax.dynamic_index_in_dim(acc, side, 0, keepdims=False)
    done = (stay + along_head(give, 2).astype(F32)).astype(BF16)
    return out, grad_q, done[:, :DH], done[:, DH:]


def solution(mesh):
    placed = (P("ctx", "head"), P("ctx", None), P("ctx", None), P("ctx", "head"), P())
    return jax.shard_map(
        shards,
        mesh=mesh,
        in_specs=placed,
        out_specs=(
            P("ctx", "head"),
            P("ctx", "head"),
            P(("ctx", "head"), None),
            P(("ctx", "head"), None),
        ),
        check_vma=False,
    )
```

```python
import math

import jax
import jax.numpy as jnp
from jax import lax
from jax.experimental import pallas as pl
from jax.experimental.pallas import tpu as pltpu
from jax.sharding import PartitionSpec as P

DH = 128
SPAN = 4
ROWS = 1024
WIN = (SPAN + 1) * ROWS
HL = 2
BQ = 512
BK = 512
SIZES = (4, 2, 1)
M = HL * BQ
QUARTER = ROWS // 4
masked_score = -1e30
F32 = jnp.float32
BF16 = jnp.bfloat16
ROW_ROW = (((1,), (1,)), ((), ()))
ROW_COL = (((1,), (0,)), ((), ()))


def dot(a, b, dims):
    return lax.dot_general(a, b, dims, preferred_element_type=F32)


def attn_kernel(sc_ref, begin_ref, q_ref, g_ref, k_hbm, v_hbm, *rest):
    mine = rest[:SPAN]
    other = rest[SPAN : 2 * SPAN]
    o_ref, dq_ref, send_ref, keep_ref = rest[2 * SPAN : 2 * SPAN + 4]
    kv, kt, vt, s_scr, dk, dv, ot_s, dq_s, g_s, q_s, stage, sem, out_sem = rest[2 * SPAN + 4 :]
    nq = ROWS // BQ
    core = sc_ref[2 * nq]
    kw = kv.at[0]
    vw = kv.at[1]
    copies = []
    for src, side, d in (
        [(k_hbm, 0, 0), (v_hbm, 1, 0)]
        + [(mine[d - 1], core, d) for d in range(1, SPAN + 1)]
        + [(other[d - 1], 1 - core, d) for d in range(1, SPAN + 1)]
    ):
        dst = kv.at[side, pl.ds((SPAN - d) * ROWS, ROWS), :]
        copies.append(pltpu.make_async_copy(src, dst, sem.at[len(copies)]))
    for c in copies:
        c.start()
    dk[...] = jnp.zeros_like(dk)
    dv[...] = jnp.zeros_like(dv)
    for c in copies:
        c.wait()

    def sweep(first, last, body, carry):
        for k in SIZES:
            count = (last - first) // k
            carry = lax.fori_loop(
                0,
                count,
                lambda i, c, first=first, k=k: body(
                    pl.multiple_of((first + k * i) * BK, BK), k * BK, c
                ),
                carry,
            )
            first = first + k * count
        return carry

    fac = 1.0 / math.sqrt(DH)
    c2 = math.log2(math.e) * fac

    @pl.loop(0, nq)
    def _(qb):
        qr = pl.ds(pl.multiple_of(qb * BQ, BQ), BQ)
        for h in range(HL):
            q_s[h * BQ : (h + 1) * BQ, :] = q_ref[qr, h * DH : (h + 1) * DH]
        diag = (SPAN * ROWS) // BK + qb
        lo = sc_ref[qb] // BK
        full = jnp.minimum((sc_ref[nq + qb] + BK - 1) // BK, diag)
        beg = jnp.concatenate([begin_ref[:, qr]] * HL, axis=1)

        def score(start, size, m, masked):
            r = pl.ds(start, size)
            kb = kw[r, :]
            s = dot(kb, q_s[...], ROW_ROW) * c2
            if masked:
                kp = start + lax.broadcasted_iota(jnp.int32, (size, M), 0)
                qp = diag * BK + (lax.broadcasted_iota(jnp.int32, (1, M), 1) & (BQ - 1))
                s = jnp.where((kp >= beg) & (kp <= qp), s, masked_score)
            s_scr[r, :] = s
            kt[:, r] = kb.T
            vt[:, r] = vw[r, :].T
            return jnp.maximum(m, jnp.max(s.reshape(size // 8, 8, M), axis=0))

        def masked_body(i, m):
            j = jnp.where(i == 0, diag, lo + i - 1)
            return score(pl.multiple_of(j * BK, BK), BK, m, True)

        m = jnp.full((8, M), masked_score, F32)
        m = lax.fori_loop(0, 1 + full - lo, masked_body, m)
        m = sweep(full, diag, lambda start, size, m: score(start, size, m, False), m)
        top = jnp.max(m, axis=0, keepdims=True)
        ot_s[...] = jnp.zeros_like(ot_s)
        dq_s[...] = jnp.zeros_like(dq_s)

        def forward_body(start, size, total):
            r = pl.ds(start, size)
            p = jnp.exp2(s_scr[r, :] - top)
            s_scr[r, :] = p
            ot_s[...] += dot(vt[:, r], p.astype(BF16), ROW_COL)
            return total + jnp.sum(p.reshape(size // 8, 8, M), axis=0)

        total = sweep(lo, diag + 1, forward_body, jnp.zeros((8, M), F32))
        inv = 1.0 / jnp.sum(total, axis=0, keepdims=True)
        out_t = ot_s[...] * inv
        g_t = jnp.concatenate([g_ref[qr, h * DH : (h + 1) * DH].T for h in range(HL)], axis=1)
        g_t = (g_t.astype(F32) * inv).astype(BF16)
        g_s[...] = g_t.T
        out_low = out_t.astype(BF16)
        for h in range(HL):
            o_ref[qr, h * DH : (h + 1) * DH] = out_low[:, h * BQ : (h + 1) * BQ].T
        delta = jnp.sum(g_t.astype(F32) * out_t, axis=0, keepdims=True)

        def backward_body(start, size, carry):
            r = pl.ds(start, size)
            dp = dot(vw[r, :], g_s[...], ROW_ROW)
            p = s_scr[r, :]
            ds = (p * (dp - delta)).astype(BF16)
            dq_s[...] += dot(kt[:, r], ds, ROW_COL)
            dk[r, :] += dot(ds, q_s[...], ROW_COL)
            dv[r, :] += dot(p.astype(BF16), g_s[...], ROW_COL)
            return carry

        sweep(lo, diag + 1, backward_body, 0)
        dq_low = (dq_s[...] * fac).astype(BF16)
        for h in range(HL):
            dq_ref[qr, h * DH : (h + 1) * DH] = dq_low[:, h * BQ : (h + 1) * BQ].T

    outs = []
    for side, dst in ((1 - core, send_ref), (core, keep_ref)):
        for w in range(SPAN + 1):
            slot = len(outs)
            for t in range(2):
                start = pl.multiple_of(w * ROWS + (2 * t + side) * QUARTER, QUARTER)
                rows = pl.ds(start, QUARTER)
                stage[slot, t, :, 0:DH] = (dk[rows, :] * fac).astype(BF16)
                stage[slot, t, :, DH : 2 * DH] = dv[rows, :].astype(BF16)
            outs.append(pltpu.make_async_copy(stage.at[slot], dst.at[w], out_sem.at[slot]))
            outs[-1].start()
    for c in outs:
        c.wait()


def attention(scalars, begin, q, g, k, v, mine, other):
    anywhere = pl.BlockSpec(memory_space=pl.ANY)
    vmem = pl.BlockSpec(memory_space=pltpu.VMEM)
    part = (SPAN + 1, 2, QUARTER, 2 * DH)
    return pl.pallas_call(
        attn_kernel,
        out_shape=(
            jax.ShapeDtypeStruct((ROWS, HL * DH), BF16),
            jax.ShapeDtypeStruct((ROWS, HL * DH), BF16),
            jax.ShapeDtypeStruct(part, BF16),
            jax.ShapeDtypeStruct(part, BF16),
        ),
        in_specs=[pl.BlockSpec(memory_space=pltpu.SMEM), vmem, vmem, vmem]
        + [anywhere] * (2 + 2 * SPAN),
        out_specs=(vmem, vmem, anywhere, anywhere),
        scratch_shapes=[
            pltpu.VMEM((2, WIN, DH), BF16),
            pltpu.VMEM((DH, WIN), BF16),
            pltpu.VMEM((DH, WIN), BF16),
            pltpu.VMEM((WIN, M), F32),
            pltpu.VMEM((WIN, DH), F32),
            pltpu.VMEM((WIN, DH), F32),
            pltpu.VMEM((DH, M), F32),
            pltpu.VMEM((DH, M), F32),
            pltpu.VMEM((M, DH), BF16),
            pltpu.VMEM((M, DH), BF16),
            pltpu.VMEM((2 * (SPAN + 1), 2, QUARTER, 2 * DH), BF16),
            pltpu.SemaphoreType.DMA((2 + 2 * SPAN,)),
            pltpu.SemaphoreType.DMA((2 * (SPAN + 1),)),
        ],
        compiler_params=pltpu.CompilerParams(vmem_limit_bytes=60 * 2**20),
        name="attn",
    )(scalars, begin, q, g, k, v, *mine, *other)


def along_ctx(x, by):
    count = lax.axis_size("ctx")
    return lax.ppermute(x, "ctx", [(i, (i + by) % count) for i in range(count)])


def along_both(x, by, flip):
    count = lax.axis_size("ctx")
    pairs = [
        (i * 4 + h, ((i + by) % count) * 4 + (h ^ flip)) for i in range(count) for h in range(4)
    ]
    return lax.ppermute(x, ("ctx", "head"), pairs)


def within_group(x, by):
    count = lax.axis_size("ctx")
    pairs = [(i, i - i % SPAN + (i + by) % SPAN) for i in range(count)]
    return lax.ppermute(x, "ctx", pairs)


def along_head(x, flip):
    return lax.ppermute(x, "head", [(i, i ^ flip) for i in range(4)])


def shards(queries, keys, values, grad_out, lengths):
    place = lax.axis_index("ctx")
    head = lax.axis_index("head")
    core = head % 2
    side = head // 2
    carried = jnp.where(core == 0, keys, values)
    mine = [along_ctx(carried, d) for d in range(1, SPAN + 1)]
    other = [along_head(x, 1) for x in mine]

    docs = jnp.arange(lengths.shape[0])
    ends = jnp.sum(jnp.where(docs[None, :] <= docs[:, None], lengths[None, :], 0), axis=1)
    own = place * ROWS + jnp.arange(ROWS, dtype=jnp.int32)
    begin = jnp.max(jnp.where(ends[:, None] <= own[None, :], ends[:, None], 0), axis=0)
    begin = begin - (place - SPAN) * ROWS
    scalars = jnp.concatenate([begin[::BQ], begin[BQ - 1 :: BQ], core[None]]).astype(jnp.int32)

    out, grad_q, send, keep = attention(
        scalars, begin.reshape(1, ROWS), queries, grad_out, keys, values, mine, other
    )
    swapped = along_head(send, 1)

    def total(d):
        return keep[SPAN - d].astype(F32) + swapped[SPAN - d].astype(F32)

    def part(x, which):
        return lax.dynamic_index_in_dim(x, which, 0, keepdims=False)

    def part_total(d, which):
        return part(keep[SPAN - d], which).astype(F32) + part(swapped[SPAN - d], which).astype(F32)

    spot = place % SPAN
    arrived = [within_group(total(d).astype(BF16), -d) for d in range(1, SPAN)]

    def summed(which, crossing):
        acc = part_total(SPAN if crossing else 0, which)
        for d in range(1, SPAN):
            fits = (spot + d >= SPAN) == crossing
            acc = acc + jnp.where(fits, part(arrived[d - 1], which).astype(F32), 0.0)
        return acc

    straight = along_both(summed(side, True).astype(BF16), -SPAN, 0)
    flipped = along_both(summed(1 - side, True).astype(BF16), -SPAN, 2)
    swapped_own = along_head(summed(1 - side, False).astype(BF16), 2)
    done = (
        summed(side, False)
        + straight.astype(F32)
        + flipped.astype(F32)
        + swapped_own.astype(F32)
    ).astype(BF16)
    return out, grad_q, done[:, :DH], done[:, DH:]


def solution(mesh):
    placed = (P("ctx", "head"), P("ctx", None), P("ctx", None), P("ctx", "head"), P())
    return jax.shard_map(
        shards,
        mesh=mesh,
        in_specs=placed,
        out_specs=(
            P("ctx", "head"),
            P("ctx", "head"),
            P(("ctx", "head"), None),
            P(("ctx", "head"), None),
        ),
        check_vma=False,
    )
```
